32 devices in a mesh: dp: 8 (over y, x, core), seq: 4 (over z).
Axes of the slice: x: 2, y: 2, z: 4, core: 2. Of those that a mesh axis runs over, the one named last changes fastest.
Arguments:
- tokens: bfloat16 [8, 2048, 768], P('dp', 'seq'), may hold values from -6 to 6
- cotangent: bfloat16 [8, 2048, 768], P('dp', 'seq'), may hold values from -6 to 6
- w_query: bfloat16 [768, 768], P(('dp', 'seq')), may hold values from -0.21875 to 0.21875
- w_key: bfloat16 [768, 768], P(('dp', 'seq')), may hold values from -0.21875 to 0.21875
- w_value: bfloat16 [768, 768], P(('dp', 'seq')), may hold values from -0.375 to 0.375
- w_output: bfloat16 [768, 768], P(('dp', 'seq')), may hold values from -0.375 to 0.375
- w_inner: bfloat16 [768, 3072], P(('dp', 'seq')), may hold values from -0.375 to 0.375
- w_outer: bfloat16 [3072, 768], P(('dp', 'seq')), may hold values from -0.1875 to 0.1875
- bias_query: bfloat16 [768], P(('dp', 'seq')), may hold values from -1.5 to 1.5
- bias_value: bfloat16 [768], P(('dp', 'seq')), may hold values from -1.5 to 1.5
- bias_output: bfloat16 [768], P(('dp', 'seq')), may hold values from -1.5 to 1.5
- bias_inner: bfloat16 [3072], P(('dp', 'seq')), may hold values from -1.5 to 1.5
- bias_outer: bfloat16 [768], P(('dp', 'seq')), may hold values from -1.5 to 1.5
- gain_input: bfloat16 [768], P(('dp', 'seq')), may hold values from 0.25 to 1.75
- bias_input: bfloat16 [768], P(('dp', 'seq')), may hold values from -1.5 to 1.5
- gain_attend: bfloat16 [768], P(('dp', 'seq')), may hold values from 0.25 to 1.75
- bias_attend: bfloat16 [768], P(('dp', 'seq')), may hold values from -1.5 to 1.5
- gain_middle: bfloat16 [768], P(('dp', 'seq')), may hold values from 0.25 to 1.75
- bias_middle: bfloat16 [768], P(('dp', 'seq')), may hold values from -1.5 to 1.5
- gain_hidden: bfloat16 [3072], P(('dp', 'seq')), may hold values from 0.25 to 1.75
- bias_hidden: bfloat16 [3072], P(('dp', 'seq')), may hold values from -1.5 to 1.5
Outputs:
- output: bfloat16 [8, 2048, 768], P('dp', 'seq')
- grad_tokens: float32 [8, 2048, 768], P('dp', 'seq')
- grad_w_query: float32 [768, 768], P(('dp', 'seq'))
- grad_w_key: float32 [768, 768], P(('dp', 'seq'))
- grad_w_value: float32 [768, 768], P(('dp', 'seq'))
- grad_w_output: float32 [768, 768], P(('dp', 'seq'))
- grad_w_inner: float32 [768, 3072], P(('dp', 'seq'))
- grad_w_outer: float32 [3072, 768], P(('dp', 'seq'))
- grad_bias_query: float32 [768], P(('dp', 'seq'))
- grad_bias_value: float32 [768], P(('dp', 'seq'))
- grad_bias_output: float32 [768], P(('dp', 'seq'))
- grad_bias_inner: float32 [3072], P(('dp', 'seq'))
- grad_bias_outer: float32 [768], P(('dp', 'seq'))
- grad_gain_input: float32 [768], P(('dp', 'seq'))
- grad_bias_input: float32 [768], P(('dp', 'seq'))
- grad_gain_attend: float32 [768], P(('dp', 'seq'))
- grad_bias_attend: float32 [768], P(('dp', 'seq'))
- grad_gain_middle: float32 [768], P(('dp', 'seq'))
- grad_bias_middle: float32 [768], P(('dp', 'seq'))
- grad_gain_hidden: float32 [3072], P(('dp', 'seq'))
- grad_bias_hidden: float32 [3072], P(('dp', 'seq'))
The draws below stay inside these ranges and needn't reach their ends.
All inputs are finite; a program needn't handle non-finite values.
Results may differ from the reference program's by a relative error of at most 0.02.
Values may be sent and summed in bfloat16 or wider, within the bound.
No kernel may reach another device: no remote copies, remote signals or barrier semaphores. Data moves between devices by JAX's collectives and lax.ppermute only.
A program may use at most 192 MiB of HBM per device.

```python
import jax
import jax.numpy as jnp
from jax import lax

D = 768
HEADS = 12
HEAD = 64
FF = 3072
SEQ_LEN = 2048
BLOCK = 256
SEQS = 8


def spiked(result, rng, source, target, blocks, factor):
    def block_of(position):
        return (jnp.arange(result.shape[position]) // (result.shape[position] // blocks)).reshape((-1,) + (1,) * (result.ndim - 1 - position))

    one_side = jax.random.permutation(rng, blocks)[block_of(target)]
    other_side = (block_of(target) + blocks // 2) % blocks
    return jnp.where((block_of(source) == one_side) | (block_of(source) == other_side), factor * result, result)


def levels(rng, shape, cuts, least, high):
    def one(axis_at, shards_of):
        heights = jax.random.uniform(jax.random.fold_in(jax.random.fold_in(rng, 6), axis_at), (shards_of,), jnp.float32, least / len(cuts), high / len(cuts))
        return jnp.repeat(jnp.exp(heights), shape[axis_at] // shards_of).reshape((-1,) + (1,) * (len(shape) - axis_at - 1))

    loudness = one(*cuts[0])
    for cut in cuts[1:]:
        loudness = loudness * one(*cut)
    return loudness


def gaussian(rng, shape, spread, bound, split=(), kind=jnp.bfloat16):
    result = jax.random.normal(rng, shape, jnp.float32) * spread
    if len(split) > 0:
        result = levels(rng, shape, split, -0.22, 0.18) * result
    return jnp.clip(result, min=-bound, max=bound).astype(kind)


def gaussian_with(stream_key, shape, width, bound, shards, heavy, held_as=jnp.bfloat16):
    drawn = width * jax.random.normal(stream_key, shape, jnp.float32)
    if shards:
        drawn = drawn * levels(stream_key, shape, shards, -0.22, 0.18)
    return jnp.clip(spiked(drawn, jax.random.fold_in(stream_key, 3), *heavy), -bound, bound).astype(held_as)


def setup_inputs(seed: int = 0) -> dict:
    splits = jax.random.split(jax.random.key(seed), 22)
    tokens = gaussian_with(splits[0], (SEQS, SEQ_LEN, D), 1.0, 6.0, ((0, 8), (1, 4)), (0, 2, 8, 2.0))
    cotangent = gaussian(splits[1], (SEQS, SEQ_LEN, D), 1.0, 6.0, ((0, 8), (1, 4)))
    w_query = gaussian(splits[2], (D, D), D ** -0.5, 0.21875, ((0, 32),))
    w_key = gaussian(splits[3], (D, D), D ** -0.5, 0.21875, ((0, 32),))
    w_value = gaussian(splits[4], (D, D), (D * 1000 // 3178) ** -0.5, 0.375, ((0, 32),))
    w_output = gaussian(splits[5], (D, D), (D * 1000 // 3178) ** -0.5, 0.375, ((0, 32),))
    w_inner = gaussian(splits[6], (D, FF), (D * 1000 // 3178) ** -0.5, 0.375, ((0, 32),))
    w_outer = gaussian(splits[7], (FF, D), (FF * 1000 // 3178) ** -0.5, 0.1875, ((0, 32),))
    bias_query = gaussian(splits[8], (D,), 0.3, 1.5, ((0, 32),))
    bias_value = gaussian(splits[9], (D,), 0.3, 1.5, ((0, 32),))
    bias_output = gaussian(splits[10], (D,), 0.3, 1.5, ((0, 32),))
    bias_inner = gaussian(splits[11], (FF,), 0.3, 1.5, ((0, 32),))
    bias_outer = gaussian(splits[12], (D,), 0.3, 1.5, ((0, 32),))
    gain_input = jnp.clip(1.0 + 0.15 * jax.random.normal(splits[13], (D,), jnp.float32), 0.25, 1.75).astype(jnp.bfloat16)
    bias_input = gaussian(splits[14], (D,), 0.3, 1.5, ((0, 32),))
    gain_attend = jnp.clip(1.0 + 0.15 * jax.random.normal(splits[15], (D,), jnp.float32), 0.25, 1.75).astype(jnp.bfloat16)
    bias_attend = gaussian(splits[16], (D,), 0.3, 1.5, ((0, 32),))
    gain_middle = jnp.clip(1.0 + 0.15 * jax.random.normal(splits[17], (D,), jnp.float32), 0.25, 1.75).astype(jnp.bfloat16)
    bias_middle = gaussian(splits[18], (D,), 0.3, 1.5, ((0, 32),))
    gain_hidden = jnp.clip(1.0 + 0.15 * jax.random.normal(splits[19], (FF,), jnp.float32), 0.25, 1.75).astype(jnp.bfloat16)
    bias_hidden = gaussian(splits[20], (FF,), 0.3, 1.5, ((0, 32),))
    return dict(tokens=tokens, cotangent=cotangent, w_query=w_query, w_key=w_key, w_value=w_value, w_output=w_output, w_inner=w_inner, w_outer=w_outer, bias_query=bias_query, bias_value=bias_value, bias_output=bias_output, bias_inner=bias_inner, bias_outer=bias_outer, gain_input=gain_input, bias_input=bias_input, gain_attend=gain_attend, bias_attend=bias_attend, gain_middle=gain_middle, bias_middle=bias_middle, gain_hidden=gain_hidden, bias_hidden=bias_hidden)


@jax.custom_vjp
def low(v):
    return lax.optimization_barrier(v.astype(jnp.bfloat16)).astype(jnp.float32)

@jax.custom_vjp
def low_back(v):
    return v

def low_keep(v):
    return (low(v), None)

def low_pass(kept, grad):
    return (grad,)

def back_keep(v):
    return (v, None)

def back_low(kept, grad):
    return (low(grad),)
low.defvjp(low_keep, low_pass)
low_back.defvjp(back_keep, back_low)
EPSILON = 1e-05
MASKED = -1e+30

def layer_norm(values, scaling, offset):
    centered = values - lax.optimization_barrier(jnp.mean(values, axis=-1, keepdims=True))
    variance = lax.optimization_barrier(jnp.mean(centered * centered, axis=-1, keepdims=True))
    return centered * lax.rsqrt(variance + EPSILON) * scaling + offset

def matmul(former, latter):
    return jnp.dot(former, latter, precision=lax.Precision.HIGHEST)

def attend_rows(query_rows, keys_all, values_all, first_row):
    count = query_rows.shape[0]
    query_pos = first_row + jnp.arange(count, dtype=jnp.int32)
    key_pos = jnp.arange(keys_all.shape[0], dtype=jnp.int32)
    visible = key_pos[None, :] // BLOCK <= query_pos[:, None] // BLOCK
    scores = jnp.einsum('qhd,khd->hqk', query_rows, keys_all, precision=lax.Precision.HIGHEST) * HEAD ** (-0.5)
    scores = low_back(scores)
    masked = jnp.where(visible[None, :, :], scores, MASKED)
    largest = lax.optimization_barrier(jnp.max(masked, axis=-1, keepdims=True))
    powered = jnp.exp(masked - largest)
    shares = low(powered / lax.optimization_barrier(jnp.sum(powered, axis=-1, keepdims=True)))
    return jnp.einsum('hqk,khd->qhd', shares, values_all, precision=lax.Precision.HIGHEST)

def forward(sequence, params):
    w_query, w_key, w_value, w_output, w_inner, w_outer, bias_query, bias_value, bias_output, bias_inner, bias_outer, gain_input, bias_input, gain_attend, bias_attend, gain_middle, bias_middle, gain_hidden, bias_hidden = params
    normed = low(layer_norm(sequence, gain_input, bias_input))
    queries = low(low_back(matmul(normed, w_query) + bias_query))
    keys_all = low(low_back(matmul(normed, w_key)))
    values_all = low(low_back(matmul(normed, w_value) + bias_value))
    block_rows = min(512, SEQ_LEN)
    count = SEQ_LEN // block_rows
    query_blocks = queries.reshape(count, block_rows, HEADS, HEAD)
    starts = jnp.arange(count, dtype=jnp.int32) * block_rows
    keys_heads = keys_all.reshape(SEQ_LEN, HEADS, HEAD)
    values_heads = values_all.reshape(SEQ_LEN, HEADS, HEAD)
    checked = jax.checkpoint(attend_rows)
    attended = lax.map(lambda pair: checked(pair[0], keys_heads, values_heads, pair[1]), (query_blocks, starts))
    attended = low_back(attended.reshape(SEQ_LEN, D))
    sub_normed = low(layer_norm(attended, gain_attend, bias_attend))
    branch = low_back(matmul(sub_normed, w_output) + bias_output)
    middle = sequence + branch
    normed_mid = low(layer_norm(middle, gain_middle, bias_middle))
    hidden_pre = low_back(matmul(normed_mid, w_inner) + bias_inner)
    hidden_low = low(layer_norm(jax.nn.gelu(hidden_pre, approximate=False), gain_hidden, bias_hidden))
    ffn_out = low_back(matmul(hidden_low, w_outer) + bias_outer)
    return middle + ffn_out

def reference(tokens, cotangent, w_query, w_key, w_value, w_output, w_inner, w_outer, bias_query, bias_value, bias_output, bias_inner, bias_outer, gain_input, bias_input, gain_attend, bias_attend, gain_middle, bias_middle, gain_hidden, bias_hidden):
    params = (w_query, w_key, w_value, w_output, w_inner, w_outer, bias_query, bias_value, bias_output, bias_inner, bias_outer, gain_input, bias_input, gain_attend, bias_attend, gain_middle, bias_middle, gain_hidden, bias_hidden)
    params = tuple((member.astype(jnp.float32) for member in params))
    sequences = tokens.astype(jnp.float32)
    cotangents = cotangent.astype(jnp.float32)

    def one_sequence(totals, pair):
        outputs, pull = jax.vjp(forward, pair[0], params)
        grad_sequence, grad_params = pull(pair[1])
        totals = tuple((total + grad for total, grad in zip(totals, grad_params)))
        return (totals, (outputs.astype(jnp.bfloat16), grad_sequence))
    zeros = tuple((jnp.zeros_like(member) for member in params))
    totals, (outputs, grads) = lax.scan(one_sequence, zeros, (sequences, cotangents))
    return (outputs, grads, totals[0], totals[1], totals[2], totals[3], totals[4], totals[5], totals[6], totals[7], totals[8], totals[9], totals[10], totals[11], totals[12], totals[13], totals[14], totals[15], totals[16], totals[17], totals[18])
```

```python
import functools

import jax
import jax.numpy as jnp
from jax import lax
from jax.experimental import pallas as pl
from jax.experimental.pallas import tpu as pltpu
from jax.sharding import PartitionSpec as P

HEAD = 64
BLOCK = 256
EPSILON = 1e-05
LOW = jnp.bfloat16
F32 = jnp.float32


def layer_norm(values, scaling, offset):
    centered = values - jnp.mean(values, axis=-1, keepdims=True)
    variance = jnp.mean(centered * centered, axis=-1, keepdims=True)
    return centered * lax.rsqrt(variance + EPSILON) * scaling + offset


def hidden_norm(hidden_pre, scaling, offset):
    return layer_norm(jax.nn.gelu(hidden_pre, approximate=False), scaling, offset)


def product(former, latter):
    return jnp.dot(former, latter, preferred_element_type=F32)


def product_left(former, latter):
    return jnp.einsum("ta,tb->ab", former, latter, preferred_element_type=F32)


def product_right(former, latter):
    return jnp.einsum("ta,ba->tb", former, latter, preferred_element_type=F32)


def column_sums(matrix):
    return jnp.sum(matrix.astype(F32), axis=0)


def dot_nt(former, latter):
    return lax.dot_general(former, latter, (((1,), (1,)), ((), ())), preferred_element_type=F32)


def dot_nn(former, latter):
    return lax.dot_general(former, latter, (((1,), (0,)), ((), ())), preferred_element_type=F32)


def attend_kernel(heads, blocks, qkv_ref, o_ref, ot_ref, lse_ref, qs, ks, vt):
    width = heads * HEAD
    for h in range(heads):
        qs[h] = qkv_ref[:, h * HEAD:(h + 1) * HEAD]
        ks[h] = qkv_ref[:, width + h * HEAD:width + (h + 1) * HEAD]
    vt[...] = qkv_ref[:, 2 * width:3 * width].T

    def row_block(i, unused):
        rows = pl.ds(pl.multiple_of(i * BLOCK, BLOCK), BLOCK)

        def pair(j, carried):
            cols = pl.ds(pl.multiple_of(j * BLOCK, BLOCK), BLOCK)
            result = []
            for h in range(heads):
                largest, totals, mixed = carried[3 * h:3 * h + 3]
                scores = dot_nt(ks[h, cols, :], qs[h, rows, :])
                newest = jnp.maximum(largest, jnp.max(scores, axis=0, keepdims=True))
                shrink = jnp.exp(largest - newest)
                powered = jnp.exp(scores - newest)
                totals = totals * shrink + jnp.sum(powered, axis=0, keepdims=True)
                mixed = mixed * shrink + dot_nn(vt[h * HEAD:(h + 1) * HEAD, cols], powered.astype(LOW))
                result += [newest, totals, mixed]
            return tuple(result)

        initial = []
        for h in range(heads):
            initial += [
                jnp.full((1, BLOCK), -jnp.inf, F32),
                jnp.zeros((1, BLOCK), F32),
                jnp.zeros((HEAD, BLOCK), F32),
            ]
        final = lax.fori_loop(0, i + 1, pair, tuple(initial))
        parts = []
        for h in range(heads):
            largest, totals, mixed = final[3 * h:3 * h + 3]
            attended = mixed / totals
            ot_ref[h * HEAD:(h + 1) * HEAD, rows] = attended
            lse_ref[h:h + 1, rows] = largest + jnp.log(totals)
            parts.append(attended)
        o_ref[rows, :] = jnp.concatenate(parts, axis=0).T.astype(LOW)
        return unused

    lax.fori_loop(0, blocks, row_block, 0)


def attend_back_kernel(heads, blocks, qkv_ref, do_ref, ot_ref, lse_ref, out_ref, qs, ks, vs, ds, kt, dk, dv):
    width = heads * HEAD
    for h in range(heads):
        qs[h] = qkv_ref[:, h * HEAD:(h + 1) * HEAD]
        ks[h] = qkv_ref[:, width + h * HEAD:width + (h + 1) * HEAD]
        vs[h] = qkv_ref[:, 2 * width + h * HEAD:2 * width + (h + 1) * HEAD]
        ds[h] = do_ref[:, h * HEAD:(h + 1) * HEAD]
    kt[...] = qkv_ref[:, width:2 * width].T
    dk[...] = jnp.zeros_like(dk)
    dv[...] = jnp.zeros_like(dv)

    def row_block(i, unused):
        rows = pl.ds(pl.multiple_of(i * BLOCK, BLOCK), BLOCK)
        inner = []
        for h in range(heads):
            grad_t = ds[h, rows, :].astype(F32).T
            inner.append(jnp.sum(grad_t * ot_ref[h * HEAD:(h + 1) * HEAD, rows], axis=0, keepdims=True))

        def pair(j, carried):
            cols = pl.ds(pl.multiple_of(j * BLOCK, BLOCK), BLOCK)
            result = []
            for h in range(heads):
                query, grad = qs[h, rows, :], ds[h, rows, :]
                shares = jnp.exp(dot_nt(ks[h, cols, :], query) - lse_ref[h:h + 1, rows])
                grad_shares = dot_nt(vs[h, cols, :], grad)
                grad_scores = (shares * (grad_shares - inner[h])).astype(LOW)
                dv[h, cols, :] += dot_nn(shares.astype(LOW), grad)
                dk[h, cols, :] += dot_nn(grad_scores, query)
                result.append(carried[h] + dot_nn(kt[h * HEAD:(h + 1) * HEAD, cols], grad_scores))
            return tuple(result)

        final = lax.fori_loop(0, i + 1, pair, tuple(jnp.zeros((HEAD, BLOCK), F32) for unused in range(heads)))
        grad_query = jnp.concatenate(final, axis=0).T * HEAD ** (-0.5)
        out_ref[rows, 0:width] = grad_query.astype(LOW)
        return unused

    lax.fori_loop(0, blocks, row_block, 0)
    for h in range(heads):
        out_ref[:, width + h * HEAD:width + (h + 1) * HEAD] = dk[h].astype(LOW)
        out_ref[:, 2 * width + h * HEAD:2 * width + (h + 1) * HEAD] = dv[h].astype(LOW)


def whole_vmem(count):
    return [pl.BlockSpec(memory_space=pltpu.VMEM)] * count


def attend_forward(qkv, heads):
    length = qkv.shape[0]
    width = heads * HEAD
    return pl.pallas_call(
        functools.partial(attend_kernel, heads, length // BLOCK),
        out_shape=(
            jax.ShapeDtypeStruct((length, width), LOW),
            jax.ShapeDtypeStruct((width, length), F32),
            jax.ShapeDtypeStruct((heads, length), F32),
        ),
        in_specs=whole_vmem(1),
        out_specs=tuple(whole_vmem(3)),
        scratch_shapes=[
            pltpu.VMEM((heads, length, HEAD), LOW),
            pltpu.VMEM((heads, length, HEAD), LOW),
            pltpu.VMEM((width, length), LOW),
        ],
        name="attend_forward",
    )(qkv)


def attend_backward(qkv, grad_attended, attended_t, logsum, heads):
    length = qkv.shape[0]
    width = heads * HEAD
    return pl.pallas_call(
        functools.partial(attend_back_kernel, heads, length // BLOCK),
        out_shape=jax.ShapeDtypeStruct((length, 3 * width), LOW),
        in_specs=whole_vmem(4),
        out_specs=whole_vmem(1)[0],
        scratch_shapes=[pltpu.VMEM((heads, length, HEAD), LOW)] * 4
        + [pltpu.VMEM((width, length), LOW)]
        + [pltpu.VMEM((heads, length, HEAD), F32)] * 2,
        name="attend_backward",
    )(qkv, grad_attended, attended_t, logsum)


def exchange(values, axis, bit):
    size = lax.axis_size(axis)
    return lax.ppermute(values, axis, [(i, i ^ (1 << bit)) for i in range(size)])


def bit_of(axis, bit):
    return (lax.axis_index(axis) >> bit) & 1


def bit_order(axis):
    count = lax.axis_size(axis).bit_length() - 1
    return count, list(range(1, count)) + [0]


def gather_tree(values, axis):
    count, order = bit_order(axis)
    for bit in order:
        other = exchange(values, axis, bit)
        first = bit_of(axis, bit) == 0
        values = jnp.stack([jnp.where(first, values, other), jnp.where(first, other, values)])
    where_is = {bit: len(order) - 1 - place for place, bit in enumerate(order)}
    axes = [where_is[bit] for bit in reversed(range(count))]
    rest = list(range(count, values.ndim))
    values = jnp.transpose(values, axes + rest)
    return values.reshape((1 << count,) + values.shape[count:])


def scatter_tree(values, axis):
    count, order = bit_order(axis)
    payload = values.shape[1:]
    values = values.reshape((2,) * count + payload)
    left = list(reversed(range(count)))
    for bit in reversed(order):
        place = left.index(bit)
        left.remove(bit)
        mine = bit_of(axis, bit)
        kept = lax.dynamic_index_in_dim(values, mine, place, keepdims=False)
        sent = lax.dynamic_index_in_dim(values, 1 - mine, place, keepdims=False)
        got = exchange(sent.astype(LOW), axis, bit)
        values = kept.astype(F32) + got.astype(F32)
    return values


def gather_neighbours(values, axis):
    size = lax.axis_size(axis)
    place = lax.axis_index(axis)
    upward = [values]
    downward = [values]
    for step in range(1, size):
        upward.append(lax.ppermute(upward[-1], axis, [(i, i + 1) for i in range(size - 1)]))
        downward.append(lax.ppermute(downward[-1], axis, [(i + 1, i) for i in range(size - 1)]))
    pieces = [values]
    for step in range(1, size):
        pieces.append(jnp.where(place >= step, upward[step], downward[size - step]))
    return pieces


def spread(values, axis):
    return lax.all_to_all(values, axis, 0, 0, tiled=True)


def per_device(
    tokens,
    cotangent,
    w_query,
    w_key,
    w_value,
    w_output,
    w_inner,
    w_outer,
    bias_query,
    bias_value,
    bias_output,
    bias_inner,
    bias_outer,
    gain_input,
    bias_input,
    gain_attend,
    bias_attend,
    gain_middle,
    bias_middle,
    gain_hidden,
    bias_hidden,
):
    seq_size, dp_size = lax.axis_size("seq"), lax.axis_size("dp")
    devices = seq_size * dp_size
    place = lax.axis_index("seq")
    groups, rows, width = tokens.shape
    count = groups * rows
    length = seq_size * rows
    all_heads = width // HEAD
    heads = groups * all_heads // seq_size
    parts = all_heads // heads
    part_width = heads * HEAD
    own_rows = w_query.shape[0]
    ff = w_inner.shape[1]
    ratio = ff // width

    packed_weights = jnp.concatenate(
        [w_output]
        + [w_inner[:, c * width:(c + 1) * width] for c in range(ratio)]
        + [w_outer, w_query, w_key, w_value],
        axis=0,
    )
    weights = lax.all_gather(packed_weights, ("dp", "seq"), axis=0, tiled=False)

    vectors = (
        bias_query, bias_value, bias_output, bias_inner, bias_outer, gain_input, bias_input,
        gain_attend, bias_attend, gain_middle, bias_middle, gain_hidden, bias_hidden,
    )
    columns = jnp.stack([w_query, w_key, w_value]).reshape(3, own_rows, parts, part_width)
    columns = jnp.transpose(columns, (2, 1, 0, 3)).reshape(parts, own_rows, 3 * part_width)
    flat = jnp.concatenate(vectors)
    extra = -(-flat.shape[0] // (3 * part_width))
    flat = jnp.pad(flat, (0, extra * 3 * part_width - flat.shape[0])).reshape(1, extra, 3 * part_width)
    first = jnp.concatenate([columns, jnp.broadcast_to(flat, (parts, extra, 3 * part_width))], axis=1)
    first = jnp.tile(first, (groups, 1, 1))
    first = gather_tree(spread(first, "seq"), "dp").reshape(devices, own_rows + extra, 3 * part_width)
    w_own = first[:, :own_rows].reshape(width, 3 * part_width)
    flat = first[:, own_rows:].reshape(devices, extra * 3 * part_width).astype(F32)
    full = []
    offset = 0
    for member in vectors:
        size = member.shape[0]
        full.append(flat[:, offset:offset + size].reshape(devices * size))
        offset += size
    (
        bq_full, bv_full, bo_full, bi_full, bu_full, gin_full, bin_full,
        gat_full, bat_full, gmi_full, bmi_full, ghi_full, bhi_full,
    ) = full

    own_group, own_part = place // parts, place % parts
    pieces = gather_neighbours(tokens, "seq")
    normed_all = jnp.zeros((seq_size, rows, width), LOW)
    for step, piece in enumerate(pieces):
        chosen = lax.dynamic_index_in_dim(piece, own_group, 0, keepdims=False) if groups > 1 else piece[0]
        normed = layer_norm(chosen.astype(F32), gin_full, bin_full).astype(LOW)
        normed_all = lax.dynamic_update_index_in_dim(normed_all, normed, (place - step) % seq_size, 0)
    normed_all = normed_all.reshape(length, width)
    bq_own = lax.dynamic_slice_in_dim(bq_full, own_part * part_width, part_width, 0)
    bv_own = lax.dynamic_slice_in_dim(bv_full, own_part * part_width, part_width, 0)
    bias_own = jnp.concatenate([bq_own, jnp.zeros_like(bq_own), bv_own])
    scale_own = jnp.concatenate(
        [jnp.full((part_width,), HEAD ** (-0.5), LOW), jnp.ones((2 * part_width,), LOW)]
    )
    qkv = (product(normed_all, w_own) + bias_own).astype(LOW) * scale_own
    attended_low, attended_t, logsum = attend_forward(qkv, heads)

    def to_rows(values, per):
        received = spread(values.reshape(seq_size, rows, per), "seq").reshape(groups, parts, rows, per)
        return received

    attended = jnp.transpose(to_rows(attended_low, part_width), (0, 2, 1, 3)).reshape(count, width).astype(F32)

    w_output_full = weights[:, :own_rows].reshape(width, width)
    at = own_rows
    w_inner_full = [weights[:, at + c * own_rows:at + (c + 1) * own_rows].reshape(width, width) for c in range(ratio)]
    w_inner_full = jnp.concatenate(w_inner_full, axis=1)
    at += ratio * own_rows
    w_outer_full = weights[:, at:at + ratio * own_rows].reshape(ff, width)
    at += ratio * own_rows
    w_qkv_full = [weights[:, at + c * own_rows:at + (c + 1) * own_rows].reshape(width, width) for c in range(3)]

    inputs = tokens.astype(F32).reshape(count, width)
    sub_low, pull_attend = jax.vjp(layer_norm, attended, gat_full, bat_full)
    sub_low = sub_low.astype(LOW)
    middle = inputs + product(sub_low, w_output_full) + bo_full
    normed_mid, pull_middle = jax.vjp(layer_norm, middle, gmi_full, bmi_full)
    normed_mid = normed_mid.astype(LOW)
    hidden_pre = product(normed_mid, w_inner_full) + bi_full
    hidden_low, pull_hidden = jax.vjp(hidden_norm, hidden_pre, ghi_full, bhi_full)
    hidden_low = hidden_low.astype(LOW)
    output = (middle + product(hidden_low, w_outer_full) + bu_full).astype(LOW)

    cotangent_flat = cotangent.reshape(count, width)
    grad_w_outer = product_left(hidden_low, cotangent_flat)
    grad_bias_outer = column_sums(cotangent_flat)
    grad_pre, grad_gain_hidden, grad_bias_hidden = pull_hidden(product_right(cotangent_flat, w_outer_full))
    grad_pre_low = grad_pre.astype(LOW)
    grad_w_inner = product_left(normed_mid, grad_pre_low)
    grad_bias_inner = column_sums(grad_pre_low)
    grad_mid_part, grad_gain_middle, grad_bias_middle = pull_middle(product_right(grad_pre_low, w_inner_full))
    grad_middle = cotangent_flat.astype(F32) + grad_mid_part
    grad_branch = grad_middle.astype(LOW)
    grad_w_output = product_left(sub_low, grad_branch)
    grad_bias_output = column_sums(grad_branch)
    grad_att, grad_gain_attend, grad_bias_attend = pull_attend(product_right(grad_branch, w_output_full))

    def packed_vectors(members, row_width):
        joined = jnp.concatenate([member.reshape(devices, -1) for member in members], axis=1)
        row_count = -(-joined.shape[1] // row_width)
        joined = jnp.pad(joined, ((0, 0), (0, row_count * row_width - joined.shape[1])))
        return joined.reshape(devices, row_count, row_width).astype(LOW)

    def unpacked(flat, sizes):
        result, offset = [], 0
        for size in sizes:
            result.append(flat[offset:offset + size])
            offset += size
        return result

    early = (
        grad_bias_output, grad_bias_inner, grad_bias_outer, grad_gain_attend, grad_bias_attend,
        grad_gain_middle, grad_bias_middle, grad_gain_hidden, grad_bias_hidden,
    )
    packed = jnp.concatenate(
        [
            grad_w_outer.astype(LOW).reshape(devices, ratio * own_rows, width),
            grad_w_inner.astype(LOW).reshape(devices, ratio * own_rows, width),
            grad_w_output.astype(LOW).reshape(devices, own_rows, width),
            packed_vectors(early, width),
        ],
        axis=1,
    )
    summed = lax.psum_scatter(packed, ("dp", "seq"), scatter_dimension=0, tiled=True)[0].astype(F32)

    grad_att_low = jnp.transpose(grad_att.astype(LOW).reshape(groups, rows, parts, part_width), (0, 2, 1, 3))
    grad_att_own = spread(grad_att_low.reshape(seq_size, rows, part_width), "seq").reshape(length, part_width)
    grad_qkv = attend_backward(qkv, grad_att_own, attended_t, logsum, heads)
    grad_w_own = product_left(normed_all, grad_qkv)

    received = to_rows(grad_qkv, 3 * part_width).reshape(groups, parts, rows, 3, part_width)
    received = jnp.transpose(received, (3, 0, 2, 1, 4)).reshape(3, count, width)
    grad_normed = (
        product_right(received[0], w_qkv_full[0])
        + product_right(received[1], w_qkv_full[1])
        + product_right(received[2], w_qkv_full[2])
    )
    grad_bias_query = column_sums(received[0])
    grad_bias_value = column_sums(received[2])
    unused, pull_input = jax.vjp(layer_norm, inputs, gin_full, bin_full)
    grad_in_part, grad_gain_input, grad_bias_input = pull_input(grad_normed)
    grad_tokens = (grad_middle + grad_in_part).reshape(groups, rows, width)

    late = (grad_bias_query, grad_bias_value, grad_gain_input, grad_bias_input)
    late_packed = packed_vectors(late, 3 * part_width)
    last = jnp.concatenate(
        [grad_w_own.astype(LOW).reshape(devices, own_rows, 3 * part_width), late_packed], axis=1
    )
    last_rows = last.shape[1]
    last = scatter_tree(last.reshape(dp_size, seq_size, last_rows, 3 * part_width), "dp")
    last = spread(last.astype(LOW), "seq").astype(F32)
    grad_own = jnp.sum(last[:, :own_rows].reshape(groups, parts, own_rows, 3, part_width), axis=0)
    grad_own = jnp.transpose(grad_own, (2, 1, 0, 3)).reshape(3, own_rows, width)
    late_flat = jnp.sum(last[:, own_rows:], axis=0).reshape(-1)
    own_ff = ratio * own_rows
    gbq, gbv, ggi, gbi = unpacked(late_flat, [own_rows] * 4)
    gbo, gbin, gbu, gga, gba, ggm, gbm, ggh, gbh = unpacked(
        summed[2 * own_ff + own_rows:].reshape(-1),
        [own_rows, own_ff, own_rows, own_rows, own_rows, own_rows, own_rows, own_ff, own_ff],
    )
    return (
        output.reshape(groups, rows, width),
        grad_tokens,
        grad_own[0],
        grad_own[1],
        grad_own[2],
        summed[2 * own_ff:2 * own_ff + own_rows],
        summed[own_ff:2 * own_ff].reshape(own_rows, ff),
        summed[:own_ff],
        gbq,
        gbv,
        gbo,
        gbin,
        gbu,
        ggi,
        gbi,
        gga,
        gba,
        ggm,
        gbm,
        ggh,
        gbh,
    )


def solution(mesh):
    rows3 = P("dp", "seq", None)
    split2 = P(("dp", "seq"), None)
    split1 = P(("dp", "seq"))
    return jax.shard_map(
        per_device,
        mesh=mesh,
        in_specs=(rows3,) * 2 + (split2,) * 6 + (split1,) * 13,
        out_specs=(rows3,) * 2 + (split2,) * 6 + (split1,) * 13,
        check_vma=False,
    )
```
